256 devices in a mesh: blk: 32 (over z, y_hi, core), grp: 8 (over y_lo, x).
Axes of the slice: x: 4, y: 4 (y_hi: 2, y_lo: 2; y = y_hi * 2 + y_lo), z: 8, core: 2. Of those that a mesh axis runs over, the one named last changes fastest.
Arguments:
- integrals: bfloat16 [128, 512, 1024], P('blk', None, 'grp'), may hold values from -1.1953125 to 1.1953125
- eps_occ: float32 [128], replicated, may hold values from -2 to -0.5
- eps_vir: float32 [512], replicated, may hold values from 0.3 to 3
- pair_mask: int32 [128, 4, 4], P('blk'), may hold values 0 or 1
Outputs:
- density: float32 [128, 512, 1024], P('blk', 'grp')
The draws below stay inside these ranges and needn't reach their ends.
All inputs are finite; a program needn't handle non-finite values. No bound on the sum of `pair_mask` on one device may be relied on, other than what follows from the above.
Results may differ from the reference program's by a relative error of at most 0.0035.
Values may be sent and summed in bfloat16 or wider, within the bound.
A program may use at most 128 MiB of HBM per device.

```python
import jax
import jax.numpy as jnp
from jax import lax

NVIR = 512
NAUX = 1024
OCC_DEV = 4
SHIFTS = 4
NOCC = 128
SLAB = 64
N_GRP = 8


def set_ends(drawn, stream_key, low, high):
    shape = drawn.shape
    place = [jax.random.randint(jax.random.fold_in(stream_key, axis), (), 0, shape[axis]) for axis in range(len(shape))]
    drawn = drawn.at[tuple(place)].set(low)
    longest = shape.index(max(shape))
    place[longest] = (place[longest] + 1) % shape[longest]
    return drawn.at[tuple(place)].set(high)


def levels(stream_key, shape, cuts, least, top_value):
    loudness, own = 1.0, jax.random.fold_in(stream_key, 6)
    for dim, blocks in cuts:
        heights = jnp.exp(jax.random.uniform(jax.random.fold_in(own, dim), (blocks,), jnp.float32, least / len(cuts), top_value / len(cuts)))
        loudness = loudness * jnp.repeat(heights, shape[dim] // blocks).reshape([-1 if axis == dim else 1 for axis in range(len(shape))])
    return loudness


def bell_draw(rng, dims, width, limit, shards=(), kind=jnp.bfloat16):
    array = jax.random.normal(rng, dims, jnp.float32) * width
    if len(shards) > 0:
        array = levels(rng, dims, shards, -0.22, 0.18) * array
    return jnp.clip(array, min=-limit, max=limit).astype(kind)


def setup_inputs(seed: int = 0) -> dict:
    streams_of = jax.random.split(jax.random.key(seed), 5)
    return {
        "integrals": bell_draw(streams_of[0], (NOCC, NVIR, NAUX), 0.18, 1.1953125, ((0, 32), (2, 8))),
        "eps_occ": jnp.clip(jax.random.uniform(streams_of[1], (NOCC,), jnp.float32, -2.0, -0.5), -2.0, -0.5),
        "eps_vir": jnp.clip(jax.random.uniform(streams_of[2], (NVIR,), jnp.float32, 0.3, 3.0), 0.3, 3.0),
        "pair_mask": set_ends((jax.random.randint(streams_of[3], (NOCC, SHIFTS, OCC_DEV), 0, 4) < 3).astype(jnp.int32), jax.random.fold_in(streams_of[3], 1), 0, 1),
    }


def reference(integrals, eps_occ, eps_vir, pair_mask):
    nblk = NOCC // OCC_DEV
    blocks = integrals.astype(jnp.float32).reshape(nblk, OCC_DEV, NVIR, NAUX)
    energies = eps_occ.reshape(nblk, OCC_DEV)
    masks = pair_mask.astype(jnp.float32).reshape(nblk, OCC_DEV, SHIFTS, OCC_DEV)
    density = jnp.zeros((nblk, OCC_DEV, NVIR, NAUX), jnp.float32)
    for shift in range(1, SHIFTS + 1):
        partner_blocks = jnp.roll(blocks, shift, axis=0)
        partner_energy = jnp.roll(energies, shift, axis=0)
        weights = masks[:, :, shift - 1, :]

        def one_block(items):
            left, right, left_e, right_e, weight = items
            coulomb = jnp.einsum("oap,lbp->olab", left, right)
            denom = left_e[:, None, None, None] + right_e[None, :, None, None] - eps_vir[None, None, :, None] - eps_vir[None, None, None, :]
            amplitude = (weight[:, :, None, None] * coulomb / denom).astype(jnp.bfloat16).astype(jnp.float32)
            own_part = jnp.einsum("olab,lbp->oap", amplitude, right)
            split_amp = amplitude.reshape(OCC_DEV, OCC_DEV, N_GRP, SLAB, NVIR)
            split_left = left.reshape(OCC_DEV, N_GRP, SLAB, NAUX)
            pieces = jnp.einsum("olgab,ogap->glbp", split_amp, split_left)
            pieces = lax.optimization_barrier(pieces.astype(jnp.bfloat16)).astype(jnp.float32)
            return own_part, jnp.sum(pieces, axis=0)

        own_part, partner_part = lax.map(one_block, (blocks, partner_blocks, energies, partner_energy, weights))
        density = density + own_part + jnp.roll(partner_part, -shift, axis=0)
    return density.reshape(NOCC, NVIR, NAUX)
```

```python
import jax
import jax.numpy as jnp
from jax import lax
from jax.experimental import pallas as pl
from jax.experimental.pallas import tpu as pltpu
from jax.sharding import PartitionSpec as P

MESH = pl.DeviceIdType.MESH
F32 = jnp.float32
BF16 = jnp.bfloat16
OCC = 4
NVIR = 512
NAUX = 1024
HALF = 256
QUART = 128
SLAB = 64
SIDE = 512
KEYS = OCC * QUART
CHUNK = 256
N_SEM = 80


def kernel(
    b_ref, eo_ref, ev_ref, mask_ref, out_ref,
    kb, qb, acc, rowb, nevb, wbuf, wsend, osend, orecv, ssem, rsem, lsem,
):
    k = lax.axis_index("blk")
    g = lax.axis_index("grp")
    nblk = lax.axis_size("blk")
    u = k % 4
    z = k // 4
    nz = nblk // 4
    yh, c = u // 2, u % 2
    yl, x = g // 4, g % 4
    y = 2 * yh + yl

    def at_y(step):
        t = (y + step) % 4
        return t, (4 * z + 2 * (t // 2) + c, 4 * (t % 2) + x)

    def at_z(step):
        return (4 * ((z + nz + step) % nz) + u, g)

    def at_x(step):
        t = (x + step) % 4
        return t, (k, 4 * yl + t)

    def at_blk(step):
        return ((k + nblk + step) % nblk, g)

    mate = (4 * z + 2 * yh + (1 - c), g)
    other_half = (k, 4 * (1 - yl) + x)
    _, up_y = at_y(1)
    _, down_y = at_y(3)

    barrier = pltpu.get_barrier_semaphore()
    peers = [at_x(1)[1], at_x(2)[1], at_x(3)[1], up_y, down_y]
    peers += [at_blk(s) for s in (1, 2, 3, 4, -1, -2, -3, -4)]
    for dev in peers:
        pl.semaphore_signal(barrier, inc=1, device_id=dev, device_id_type=MESH)
    pl.semaphore_wait(barrier, len(peers))

    sent = []

    def descriptor(i, src, dst, dev):
        return pltpu.make_async_remote_copy(
            src_ref=src, dst_ref=dst, send_sem=ssem.at[i], recv_sem=rsem.at[i],
            device_id=dev, device_id_type=MESH,
        )

    def send(i, src, dst, dev):
        copy = descriptor(i, src, dst, dev)
        copy.start()
        sent.append(copy)

    def arrived(i, ref):
        descriptor(i, ref, ref, mate).wait_recv()

    counter = iter(range(N_SEM))

    def new(n):
        return [next(counter) for _ in range(n)]

    cols = pl.ds(pl.multiple_of(g * 128, 128), 128)
    q_rows = lambda half: pl.ds(pl.multiple_of(half * HALF, HALF), HALF)
    k_rows = lambda quart: pl.ds(pl.multiple_of(quart * QUART, QUART), QUART)

    def unit(plane, t, o0, no):
        slot = 4 * (plane + 1) + 2 * (t // 2) + c
        return kb.at[slot, pl.ds(o0, no), :, pl.ds(pl.multiple_of((t % 2) * SIDE, SIDE), SIDE)]

    s1 = new(3)
    for t in (1, 2, 3):
        xt, dev = at_x(t)
        send(s1[t - 1], b_ref.at[:, k_rows(xt), :], kb.at[4 + u, :, :, cols], dev)
    l1 = pltpu.make_async_copy(b_ref.at[:, k_rows(x), :], kb.at[4 + u, :, :, cols], lsem.at[0])
    l1.start()
    (q1,) = new(1)
    send(q1, b_ref.at[:, q_rows(1 - yl), :], qb.at[:, :, cols], other_half)
    q2 = new(3)
    for t in (1, 2, 3):
        send(q2[t - 1], b_ref.at[:, q_rows(yl), :], qb.at[:, :, cols], at_x(t)[1])
    l2 = pltpu.make_async_copy(b_ref.at[:, q_rows(yl), :], qb.at[:, :, cols], lsem.at[1])
    l2.start()

    for s in range(1, 5):
        for o in range(OCC):
            for l in range(OCC):
                lanes = pl.ds(l * QUART, QUART)
                wbuf[4 - s, pl.ds(o, 1), lanes] = jnp.full((1, QUART), mask_ref[o, s - 1, l].astype(F32), F32)
                wsend[s - 1, pl.ds(o, 1), lanes] = jnp.full((1, QUART), mask_ref[l, s - 1, o].astype(F32), F32)
    wsem = new(4)
    for s in range(1, 5):
        send(wsem[s - 1], wsend.at[s - 1], wbuf.at[4 + s], at_blk(-s))
    evq = ev_ref[pl.ds(x, 1), :]
    for d in range(9):
        j = (k + nblk + d - 4) % nblk
        for o in range(OCC):
            for l in range(OCC):
                e = eo_ref[OCC * k + o] + eo_ref[OCC * j + l]
                rowb[d, pl.ds(o, 1), pl.ds(l * QUART, QUART)] = e - evq
    for h in range(2):
        row = ev_ref[pl.ds(2 * yl + h, 1), :]
        nevb[pl.ds(h * 128, 128), :] = jnp.transpose(jnp.broadcast_to(row, (128, 128)))
    acc[...] = jnp.zeros_like(acc)

    l1.wait()
    for t in (1, 2, 3):
        xt, _ = at_x(4 - t)
        arrived(s1[t - 1], kb.at[4 + u, :, :, pl.ds(pl.multiple_of((4 * yl + xt) * 128, 128), 128)])

    a1 = new(2)
    b1y = new(2)
    b1z = new(2)
    a3o = new(2)
    a3 = new(6)
    a2 = new(2)
    b2 = new(4)
    b3 = new(6)
    dd = new(24)
    dd_i = iter(dd)
    mates = []

    def to_mate(plane, step, o0, no):
        t, _ = at_y(step)
        i = next(dd_i)
        ref = unit(plane, t, o0, no)
        send(i, ref, ref, mate)
        slot = 4 * (plane + 1) + 2 * (t // 2) + (1 - c)
        half = pl.ds(pl.multiple_of((t % 2) * SIDE, SIDE), SIDE)
        mates.append((i, kb.at[slot, pl.ds(o0, no), :, half]))

    def y_copy(i, plane, origin, o0, no, dev):
        ref = unit(plane, origin, o0, no)
        send(i, ref, ref, dev)

    def z_copy(i, origin, o0, no, step):
        send(i, unit(0, origin, o0, no), unit(-step, origin, o0, no), at_z(step))

    y_up, _ = at_y(1)
    y_dn, _ = at_y(3)
    y_far, _ = at_y(2)
    for i, dev in zip(a1, (up_y, down_y)):
        y_copy(i, 0, y, 0, 2, dev)
    for i, step in zip(b1z, (1, -1)):
        z_copy(i, y, 2, 2, step)
    for i, step in zip(a3o, (1, -1)):
        z_copy(i, y, 0, 2, step)
    for i, dev in zip(b1y, (up_y, down_y)):
        y_copy(i, 0, y, 2, 2, dev)
    to_mate(0, 0, 0, 2)
    to_mate(0, 0, 2, 2)

    other_cols = pl.ds(pl.multiple_of((4 * (1 - yl) + x) * 128, 128), 128)
    arrived(q1, qb.at[:, :, other_cols])
    q3 = new(3)
    for t in (1, 2, 3):
        ref = qb.at[:, :, other_cols]
        send(q3[t - 1], ref, ref, at_x(t)[1])

    arrived(a1[0], unit(0, y_dn, 0, 2))
    y_copy(a2[0], 0, y_dn, 0, 1, up_y)
    z_copy(a3[0], y_dn, 0, 2, 1)
    z_copy(a3[1], y_dn, 0, 2, -1)
    to_mate(0, 3, 0, 2)
    arrived(a1[1], unit(0, y_up, 0, 2))
    y_copy(a2[1], 0, y_up, 1, 1, down_y)
    z_copy(a3[2], y_up, 0, 2, 1)
    z_copy(a3[3], y_up, 0, 2, -1)
    to_mate(0, 1, 0, 2)
    for n, plane in enumerate((-1, 1)):
        arrived(b1z[n], unit(plane, y, 2, 2))
        y_copy(b2[2 * n], plane, y, 2, 2, up_y)
        y_copy(b2[2 * n + 1], plane, y, 2, 2, down_y)
        to_mate(plane, 0, 2, 2)
    arrived(b1y[0], unit(0, y_dn, 2, 2))
    y_copy(b3[0], 0, y_dn, 2, 1, up_y)
    to_mate(0, 3, 2, 2)
    arrived(b1y[1], unit(0, y_up, 2, 2))
    y_copy(b3[1], 0, y_up, 3, 1, down_y)
    to_mate(0, 1, 2, 2)

    l2.wait()
    for t in (1, 2, 3):
        xt, _ = at_x(4 - t)
        arrived(q2[t - 1], qb.at[:, :, pl.ds(pl.multiple_of((4 * yl + xt) * 128, 128), 128)])
        arrived(q3[t - 1], qb.at[:, :, pl.ds(pl.multiple_of((4 * (1 - yl) + xt) * 128, 128), 128)])

    arrived(a2[0], unit(0, y_far, 0, 1))
    arrived(a2[1], unit(0, y_far, 1, 1))
    z_copy(a3[4], y_far, 0, 2, 1)
    z_copy(a3[5], y_far, 0, 2, -1)
    to_mate(0, 2, 0, 2)
    for n, plane in enumerate((-1, 1)):
        arrived(b2[2 * n], unit(plane, y_dn, 2, 2))
        y_copy(b3[2 + 2 * n], plane, y_dn, 2, 1, up_y)
        to_mate(plane, 3, 2, 2)
        arrived(b2[2 * n + 1], unit(plane, y_up, 2, 2))
        y_copy(b3[3 + 2 * n], plane, y_up, 3, 1, down_y)
        to_mate(plane, 1, 2, 2)
    arrived(b3[0], unit(0, y_far, 2, 1))
    arrived(b3[1], unit(0, y_far, 3, 1))
    to_mate(0, 2, 2, 2)

    def arrive_mates(n):
        for i, ref in mates[:n]:
            arrived(i, ref)
        del mates[:n]

    for s in range(1, 5):
        arrived(wsem[s - 1], wbuf.at[4 + s])

    def block(slot, a0):
        d = slot - u
        keys = kb[slot].reshape(KEYS, NAUX)
        q = qb[:, pl.ds(a0, CHUNK), :].reshape(OCC * CHUNK, NAUX)
        s = lax.dot_general(q, keys, (((1,), (1,)), ((), ())), preferred_element_type=F32)
        nev = nevb[pl.ds(a0, CHUNK), :]
        nev = jnp.concatenate([nev] * OCC, axis=1)
        parts = []
        for o in range(OCC):
            den = rowb[d, pl.ds(o, 1), :] - nev
            w = wbuf[d, pl.ds(o, 1), :]
            parts.append((s[o * CHUNK : (o + 1) * CHUNK] * w / den).astype(BF16))
        amp = jnp.concatenate(parts, axis=0)
        acc[:, pl.ds(a0, CHUNK), :] += jnp.dot(amp, keys, preferred_element_type=F32).reshape(OCC, CHUNK, NAUX)

    def blocks(slot_of, n):
        def body(i, _):
            block(slot_of(i // (HALF // CHUNK)), pl.multiple_of((i % (HALF // CHUNK)) * CHUNK, CHUNK))
            return 0
        lax.fori_loop(0, n * (HALF // CHUNK), body, 0)

    arrive_mates(len(mates))
    blocks(lambda i: 4 + (u + 1 + i) % 4, 3)

    for n, step in enumerate((1, -1)):
        plane = -step
        arrived(a3o[n], unit(plane, y, 0, 2))
        to_mate(plane, 0, 0, 2)
        arrived(a3[n], unit(plane, y_dn, 0, 2))
        to_mate(plane, 3, 0, 2)
        arrived(a3[2 + n], unit(plane, y_up, 0, 2))
        to_mate(plane, 1, 0, 2)
        arrived(a3[4 + n], unit(plane, y_far, 0, 2))
        to_mate(plane, 2, 0, 2)
        arrived(b3[2 + 2 * n], unit(plane, y_far, 2, 1))
        arrived(b3[3 + 2 * n], unit(plane, y_far, 3, 1))
        to_mate(plane, 2, 2, 2)
    arrive_mates(len(mates))

    def outer(i):
        p = (u + i) % 4
        near = jnp.where(p >= u, p, 8 + p)
        return jnp.where(i == 4, 8 + u, near)

    blocks(outer, 5)

    osem = new(3)
    for t in (2, 1, 3):
        xt, dev = at_x(t)
        rows = pl.ds(pl.multiple_of(xt * SLAB, SLAB), SLAB)
        osend[t - 1] = acc[:, rows, :].astype(BF16)
        send(osem[t - 1], osend.at[t - 1], orecv.at[t - 1], dev)
    rows = pl.ds(pl.multiple_of(x * SLAB, SLAB), SLAB)
    total = acc[:, rows, :]
    for t in (1, 3, 2):
        arrived(osem[t - 1], orecv.at[t - 1])
        total = total + orecv[t - 1].astype(F32)
    out_ref[...] = total
    for copy in sent:
        copy.wait_send()


def shards(integrals, eps_occ, eps_vir, pair_mask):
    vmem = pl.BlockSpec(memory_space=pltpu.VMEM)
    smem = pl.BlockSpec(memory_space=pltpu.SMEM)
    return pl.pallas_call(
        kernel,
        out_shape=jax.ShapeDtypeStruct((OCC, SLAB, NAUX), F32),
        in_specs=[pl.BlockSpec(memory_space=pl.ANY), smem, vmem, smem],
        out_specs=vmem,
        scratch_shapes=[
            pltpu.VMEM((12, OCC, QUART, NAUX), BF16),
            pltpu.VMEM((OCC, HALF, NAUX), BF16),
            pltpu.VMEM((OCC, HALF, NAUX), F32),
            pltpu.VMEM((9, 8, KEYS), F32),
            pltpu.VMEM((HALF, 128), F32),
            pltpu.VMEM((9, 8, KEYS), F32),
            pltpu.VMEM((4, 8, KEYS), F32),
            pltpu.VMEM((3, OCC, SLAB, NAUX), BF16),
            pltpu.VMEM((3, OCC, SLAB, NAUX), BF16),
            pltpu.SemaphoreType.DMA((N_SEM,)),
            pltpu.SemaphoreType.DMA((N_SEM,)),
            pltpu.SemaphoreType.DMA((2,)),
        ],
        compiler_params=pltpu.CompilerParams(
            collective_id=0, has_side_effects=True, vmem_limit_bytes=56 * 1024 * 1024
        ),
        name="amplitudes",
    )(integrals, eps_occ, eps_vir.reshape(4, 128), pair_mask)


def solution(mesh):
    return jax.shard_map(
        shards,
        mesh=mesh,
        in_specs=(P("blk", None, "grp"), P(), P(), P("blk", None, None)),
        out_specs=P("blk", "grp", None),
        check_vma=False,
    )
```

```python
import jax
import jax.numpy as jnp
from jax import lax
from jax.experimental import pallas as pl
from jax.experimental.pallas import tpu as pltpu
from jax.sharding import PartitionSpec as P

MESH = pl.DeviceIdType.MESH
F32 = jnp.float32
BF16 = jnp.bfloat16
OCC = 4
NVIR = 512
NAUX = 1024
HALF = 256
QUART = 128
SLAB = 64
SIDE = 512
KEYS = OCC * QUART
N_SEM = 72


def kernel(
    b_ref, eo_ref, ev_ref, mask_ref, out_ref,
    kb, qb, acc, rowb, nevb, wbuf, wsend, osend, orecv, ssem, rsem, lsem,
):
    k = lax.axis_index("blk")
    g = lax.axis_index("grp")
    nblk = lax.axis_size("blk")
    u = k % 4
    z = k // 4
    nz = nblk // 4
    yh, c = u // 2, u % 2
    yl, x = g // 4, g % 4

    def at_z(step):
        return (4 * ((z + nz + step) % nz) + u, g)

    def at_x(step):
        return (k, 4 * yl + (x + step) % 4)

    def at_blk(step):
        return ((k + nblk + step) % nblk, g)

    mate = (k + 1 - 2 * c, g)
    lo = (k, 4 * (1 - yl) + x)
    hi = (4 * z + (u + 2) % 4, 4 * (1 - yl) + x)
    right, left = at_x(1), at_x(3)

    barrier = pltpu.get_barrier_semaphore()
    peers = [at_x(1), at_x(2), at_x(3), lo, hi]
    peers += [at_blk(s) for s in (1, 2, 3, 4, -1, -2, -3, -4)]
    for dev in peers:
        pl.semaphore_signal(barrier, inc=1, device_id=dev, device_id_type=MESH)
    pl.semaphore_wait(barrier, len(peers))

    sent = []
    sems = {}

    def descriptor(name, src, dst, dev):
        i = sems.setdefault(name, len(sems))
        return pltpu.make_async_remote_copy(
            src_ref=src, dst_ref=dst, send_sem=ssem.at[i], recv_sem=rsem.at[i],
            device_id=dev, device_id_type=MESH,
        )

    def send(name, src, dst, dev):
        copy = descriptor(name, src, dst, dev)
        copy.start()
        sent.append(copy)

    def arrived(name, ref):
        descriptor(name, ref, ref, mate).wait_recv()

    def part(start, size):
        return pl.ds(pl.multiple_of(start, size), size)

    own, mown = 4 + u, 5 + u - 2 * c
    mu = mown - 4
    s2, s4 = 2 - 4 * yh, 4 - 8 * yh
    below, above = u, 8 + u
    cross, mcross = own + s2, mown + s2
    diag, mdiag = own - s2, mown - s2
    dsend = own + s4
    zshare, mzshare = u + 8 * (1 - c), mu + 8 * c

    def unit(slot, half, pr):
        return kb.at[slot, pl.ds(2 * pr, 2), :, part(half * SIDE, SIDE)]

    def whole(slot, pr):
        return kb.at[slot, pl.ds(2 * pr, 2)]

    def slice_of(t):
        return part(((4 * yl) + (x + t) % 4) * 128, 128)

    def other_slice_of(t):
        return part((4 * (1 - yl) + (x + t) % 4) * 128, 128)

    cols = slice_of(0)

    def q_part(h):
        return pl.ds(h * 128, 128)

    local = []
    for pr in range(2):
        for t in (1, 3, 2):
            rows = part((x + t) % 4 * QUART, QUART)
            send(("s1", pr, t), b_ref.at[pl.ds(2 * pr, 2), rows, :], kb.at[own, pl.ds(2 * pr, 2), :, cols], at_x(t))
        rows = part(x * QUART, QUART)
        copy = pltpu.make_async_copy(b_ref.at[pl.ds(2 * pr, 2), rows, :], kb.at[own, pl.ds(2 * pr, 2), :, cols], lsem.at[pr])
        copy.start()
        local.append(copy)
    for h in range(2):
        send(("q1", h), b_ref.at[:, part((1 - yl) * HALF + h * 128, 128), :], qb.at[:, q_part(h), cols], lo)

    def queries(h):
        for t in (1, 3, 2):
            send(("q2", h, t), b_ref.at[:, part(yl * HALF + h * 128, 128), :], qb.at[:, q_part(h), cols], at_x(t))

    def queries_other(h):
        ref = qb.at[:, q_part(h), other_slice_of(0)]
        arrived(("q1", h), ref)
        for t in (1, 3, 2):
            send(("q3", h, t), ref, ref, at_x(t))

    def queries_arrived(h):
        local[2 + h].wait()
        for t in (1, 3, 2):
            arrived(("q2", h, t), qb.at[:, q_part(h), slice_of(4 - t)])
            arrived(("q3", h, t), qb.at[:, q_part(h), other_slice_of(4 - t)])

    queries(0)
    for h in range(2):
        copy = pltpu.make_async_copy(b_ref.at[:, part(yl * HALF + h * 128, 128), :], qb.at[:, q_part(h), cols], lsem.at[2 + h])
        copy.start()
        local.append(copy)

    for s in range(1, 5):
        for o in range(OCC):
            for l in range(OCC):
                lanes = pl.ds(l * QUART, QUART)
                wbuf[4 - s, pl.ds(o, 1), lanes] = jnp.full((1, QUART), mask_ref[o, s - 1, l].astype(F32), F32)
                wsend[s - 1, pl.ds(o, 1), lanes] = jnp.full((1, QUART), mask_ref[l, s - 1, o].astype(F32), F32)
    for s in range(1, 5):
        send(("w", s), wsend.at[s - 1], wbuf.at[4 + s], at_blk(-s))
    evq = ev_ref[pl.ds(x, 1), :]
    for d in range(9):
        j = (k + nblk + d - 4) % nblk
        for o in range(OCC):
            for l in range(OCC):
                e = eo_ref[OCC * k + o] + eo_ref[OCC * j + l]
                rowb[d, pl.ds(o, 1), pl.ds(l * QUART, QUART)] = e - evq
    for h in range(2):
        row = ev_ref[pl.ds(2 * yl + h, 1), :]
        nevb[pl.ds(h * 128, 128), :] = jnp.transpose(jnp.broadcast_to(row, (128, 128)))
    acc[...] = jnp.zeros_like(acc)

    def own_ready(pr):
        local[pr].wait()
        for t in (1, 3, 2):
            arrived(("s1", pr, t), kb.at[own, pl.ds(2 * pr, 2), :, slice_of(4 - t)])
        ref = unit(own, yl, pr)
        send(("hi", pr), ref, ref, hi)
        send(("lo", pr), ref, ref, lo)
        for step in (1, -1):
            send(("z", step, pr), ref, unit(own - 4 * step, yl, pr), at_z(step))

    def to_mate(name, slot, pr):
        send((name, pr), whole(slot, pr), whole(slot, pr), mate)

    def lo_ready(pr):
        ref = unit(own, 1 - yl, pr)
        arrived(("lo", pr), ref)
        for step in (1, -1):
            send(("zz", step, pr), ref, unit(own - 4 * step, 1 - yl, pr), at_z(step))
        to_mate("mown", own, pr)

    def hi_ready(pr):
        ref = unit(cross, 1 - yl, pr)
        arrived(("hi", pr), ref)
        send(("loc", pr), ref, ref, lo)

    def z_ready(pr):
        for step in (1, -1):
            arrived(("z", step, pr), unit(own - 4 * step, yl, pr))
        ref = unit(dsend, yl, pr)
        send(("hid", pr), ref, ref, hi)

    def zz_ready(pr):
        for step in (1, -1):
            arrived(("zz", step, pr), unit(own - 4 * step, 1 - yl, pr))
        if pr == 1:
            ref = unit(dsend, 1 - yl, pr)
            send(("hie", pr), ref, ref, hi)
        to_mate("mz", zshare, pr)

    def cross_ready(pr):
        arrived(("loc", pr), unit(cross, yl, pr))
        to_mate("mcross", cross, pr)

    def hid_ready():
        ref = unit(diag, 1 - yl, 0)
        arrived(("hid", 0), ref)
        send(("lod", 0), ref, ref, lo)

    def diag_ready(pr):
        if pr == 0:
            arrived(("lod", 0), unit(diag, yl, 0))
        else:
            arrived(("hid", 1), unit(diag, 1 - yl, 1))
            arrived(("hie", 1), unit(diag, yl, 1))
        to_mate("mdiag", diag, pr)

    def from_mate(name, slot, pr):
        arrived((name, pr), whole(slot, pr))

    def pick(i, values):
        value = values[-1]
        for n in range(len(values) - 2, -1, -1):
            value = jnp.where(i == n, values[n], value)
        return value

    def compute(units, a0, na):
        def body(i, _):
            rows = pl.ds(a0, na)
            q = qb[:, rows, :].reshape(OCC * na, NAUX)
            nev = nevb[rows, :]
            nev = jnp.concatenate([nev] * 2, axis=1)
            total = None
            for n in range(2):
                slot = pick(i, [unit[n][0] for unit in units])
                pr = pick(i, [unit[n][1] for unit in units])
                d = slot - u
                keys = kb[slot, pl.ds(2 * pr, 2)].reshape(2 * QUART, NAUX)
                s = lax.dot_general(q, keys, (((1,), (1,)), ((), ())), preferred_element_type=F32)
                lanes = part(pr * 256, 256)
                amps = []
                for o in range(OCC):
                    den = rowb[d, pl.ds(o, 1), lanes] - nev
                    w = wbuf[d, pl.ds(o, 1), lanes]
                    amps.append((s[o * na : (o + 1) * na] * w / den).astype(BF16))
                amp = jnp.concatenate(amps, axis=0)
                term = jnp.dot(amp, keys, preferred_element_type=F32)
                total = term if total is None else total + term
            acc[:, rows, :] += total.reshape(OCC, na, NAUX)
            return 0

        lax.fori_loop(0, len(units), body, 0)

    u0 = ((mown, 0), (mown, 1))
    u1 = ((cross, 0), (below, 0))
    u2 = ((above, 0), (mzshare, 0))
    u3 = ((mcross, 0), (cross, 1))
    u4 = ((below, 1), (above, 1))
    u5 = ((mzshare, 1), (mcross, 1))
    u6 = ((diag, 0), (diag, 1))
    u7 = ((mdiag, 0), (mdiag, 1))

    own_ready(0)
    queries_other(0)
    own_ready(1)
    queries(1)
    queries_other(1)
    lo_ready(0)
    hi_ready(0)
    z_ready(0)
    lo_ready(1)
    hi_ready(1)
    z_ready(1)
    for s in range(1, 5):
        arrived(("w", s), wbuf.at[4 + s])
    from_mate("mown", mown, 0)
    from_mate("mown", mown, 1)
    queries_arrived(0)
    compute([u0], 0, 128)
    zz_ready(0)
    cross_ready(0)
    hid_ready()
    compute([u1], 0, 128)
    from_mate("mz", mzshare, 0)
    from_mate("mcross", mcross, 0)
    compute([u2], 0, 128)
    zz_ready(1)
    cross_ready(1)
    queries_arrived(1)
    compute([u0, u1, u2], 128, 128)
    diag_ready(0)
    from_mate("mz", mzshare, 1)
    from_mate("mcross", mcross, 1)
    compute([u3, u4], 0, 256)
    diag_ready(1)
    compute([u5], 0, 256)
    for pr in range(2):
        from_mate("mdiag", mdiag, pr)
    late = [u6, u7]

    def slab(t):
        return part((x + t) % 4 * SLAB, SLAB)

    def finish(t):
        compute(late, pl.multiple_of((x + t) % 4 * SLAB, SLAB), SLAB)

    def push(n, value, dev):
        osend[n] = value.astype(BF16)
        send(("o", n), osend.at[n], orecv.at[n], dev)

    first_two, last_two = slice(0, 2), slice(2, 4)
    finish(2)
    push(0, acc[first_two, slab(2), :], right)
    push(1, acc[last_two, slab(2), :], left)
    finish(1)
    push(2, acc[last_two, slab(1), :], right)
    finish(3)
    push(3, acc[first_two, slab(3), :], left)
    arrived(("o", 0), orecv.at[0])
    push(4, acc[first_two, slab(1), :] + orecv[0].astype(F32), right)
    arrived(("o", 1), orecv.at[1])
    push(5, acc[last_two, slab(3), :] + orecv[1].astype(F32), left)
    finish(0)
    for n in (2, 3):
        arrived(("o", n), orecv.at[n])
    arrived(("o", 4), orecv.at[4])
    out_ref[first_two] = acc[first_two, slab(0), :] + orecv[3].astype(F32) + orecv[4].astype(F32)
    arrived(("o", 5), orecv.at[5])
    out_ref[last_two] = acc[last_two, slab(0), :] + orecv[2].astype(F32) + orecv[5].astype(F32)
    for copy in sent:
        copy.wait_send()


def shards(integrals, eps_occ, eps_vir, pair_mask):
    vmem = pl.BlockSpec(memory_space=pltpu.VMEM)
    smem = pl.BlockSpec(memory_space=pltpu.SMEM)
    return pl.pallas_call(
        kernel,
        out_shape=jax.ShapeDtypeStruct((OCC, SLAB, NAUX), F32),
        in_specs=[pl.BlockSpec(memory_space=pl.ANY), smem, vmem, smem],
        out_specs=vmem,
        scratch_shapes=[
            pltpu.VMEM((12, OCC, QUART, NAUX), BF16),
            pltpu.VMEM((OCC, HALF, NAUX), BF16),
            pltpu.VMEM((OCC, HALF, NAUX), F32),
            pltpu.VMEM((9, 8, KEYS), F32),
            pltpu.VMEM((HALF, 128), F32),
            pltpu.VMEM((9, 8, KEYS), F32),
            pltpu.VMEM((4, 8, KEYS), F32),
            pltpu.VMEM((6, 2, SLAB, NAUX), BF16),
            pltpu.VMEM((6, 2, SLAB, NAUX), BF16),
            pltpu.SemaphoreType.DMA((N_SEM,)),
            pltpu.SemaphoreType.DMA((N_SEM,)),
            pltpu.SemaphoreType.DMA((4,)),
        ],
        compiler_params=pltpu.CompilerParams(
            collective_id=0, has_side_effects=True, vmem_limit_bytes=56 * 1024 * 1024
        ),
        name="amplitudes",
    )(integrals, eps_occ, eps_vir.reshape(4, 128), pair_mask)


def solution(mesh):
    return jax.shard_map(
        shards,
        mesh=mesh,
        in_specs=(P("blk", None, "grp"), P(), P(), P("blk", None, None)),
        out_specs=P("blk", "grp", None),
        check_vma=False,
    )
```

```python
import jax
import jax.numpy as jnp
from jax import lax
from jax.experimental import pallas as pl
from jax.experimental.pallas import tpu as pltpu
from jax.sharding import PartitionSpec as P

MESH = pl.DeviceIdType.MESH
F32 = jnp.float32
BF16 = jnp.bfloat16
OCC = 4
NVIR = 512
NAUX = 1024
HALF = 256
QUART = 128
SLAB = 64
SIDE = 512
KEYS = OCC * QUART
N_SEM = 96


def kernel(
    b_ref, eo_ref, ev_ref, mask_ref, out_ref,
    kb, qb, acc, rowb, nevb, wbuf, wsend, osend, orecv, ssem, rsem, lsem,
):
    k = lax.axis_index("blk")
    g = lax.axis_index("grp")
    nblk = lax.axis_size("blk")
    u = k % 4
    z = k // 4
    nz = nblk // 4
    yh, c = u // 2, u % 2
    yl, x = g // 4, g % 4

    def at_z(step):
        return (4 * ((z + nz + step) % nz) + u, g)

    def at_x(step):
        return (k, 4 * yl + (x + step) % 4)

    def at_blk(step):
        return ((k + nblk + step) % nblk, g)

    mate = (k + 1 - 2 * c, g)
    lo = (k, 4 * (1 - yl) + x)
    hi = (4 * z + (u + 2) % 4, 4 * (1 - yl) + x)
    right, left = at_x(1), at_x(3)

    barrier = pltpu.get_barrier_semaphore()
    peers = [at_x(1), at_x(2), at_x(3), lo, hi]
    peers += [at_blk(s) for s in (1, 2, 3, 4, -1, -2, -3, -4)]
    for dev in peers:
        pl.semaphore_signal(barrier, inc=1, device_id=dev, device_id_type=MESH)
    pl.semaphore_wait(barrier, len(peers))

    sent = []
    sems = {}

    def descriptor(name, src, dst, dev):
        i = sems.setdefault(name, len(sems))
        return pltpu.make_async_remote_copy(
            src_ref=src, dst_ref=dst, send_sem=ssem.at[i], recv_sem=rsem.at[i],
            device_id=dev, device_id_type=MESH,
        )

    def send(name, src, dst, dev):
        copy = descriptor(name, src, dst, dev)
        copy.start()
        sent.append(copy)

    def arrived(name, ref):
        descriptor(name, ref, ref, mate).wait_recv()

    def part(start, size):
        return pl.ds(pl.multiple_of(start, size), size)

    own, mown = 4 + u, 5 + u - 2 * c
    mu = mown - 4
    s2, s4 = 2 - 4 * yh, 4 - 8 * yh
    below, above = u, 8 + u
    cross, mcross = own + s2, mown + s2
    diag, mdiag = own - s2, mown - s2
    dsend = own + s4
    zshare, mzshare = u + 8 * (1 - c), mu + 8 * c

    def unit(slot, half, pr):
        return kb.at[slot, pl.ds(2 * pr, 2), :, part(half * SIDE, SIDE)]

    def whole(slot, pr):
        return kb.at[slot, pl.ds(2 * pr, 2)]

    def slice_of(t):
        return part(((4 * yl) + (x + t) % 4) * 128, 128)

    def other_slice_of(t):
        return part((4 * (1 - yl) + (x + t) % 4) * 128, 128)

    cols = slice_of(0)

    local = []
    for pr in range(2):
        for t in (1, 3, 2):
            rows = part((x + t) % 4 * QUART, QUART)
            send(("s1", pr, t), b_ref.at[pl.ds(2 * pr, 2), rows, :], kb.at[own, pl.ds(2 * pr, 2), :, cols], at_x(t))
        rows = part(x * QUART, QUART)
        copy = pltpu.make_async_copy(b_ref.at[pl.ds(2 * pr, 2), rows, :], kb.at[own, pl.ds(2 * pr, 2), :, cols], lsem.at[pr])
        copy.start()
        local.append(copy)
    for s in range(4):
        send(("q1", s), b_ref.at[:, part((1 - yl) * HALF + s * SLAB, SLAB), :], qb.at[:, pl.ds(s * SLAB, SLAB), cols], lo)

    def slab_of(place):
        return part(place % 4 * SLAB, SLAB)

    def slab(t):
        return slab_of(x + t)

    def queries(turn):
        for t in (1, 3, 2):
            rows = part(yl * HALF + (x + t + turn) % 4 * SLAB, SLAB)
            send(("q2", turn, t), b_ref.at[:, rows, :], qb.at[:, slab_of(x + t + turn), cols], at_x(t))

    def queries_other(turn):
        for t in (1, 3, 2):
            ref = qb.at[:, slab_of(x + t + turn), other_slice_of(0)]
            send(("q3", turn, t), ref, ref, at_x(t))

    def queries_arrived(turn):
        for t in (1, 3, 2):
            arrived(("q2", turn, t), qb.at[:, slab(turn), slice_of(4 - t)])
            arrived(("q3", turn, t), qb.at[:, slab(turn), other_slice_of(4 - t)])

    queries(2)
    copy = pltpu.make_async_copy(b_ref.at[:, part(yl * HALF, HALF), :], qb.at[:, :, cols], lsem.at[2])
    copy.start()
    local.append(copy)

    for s in range(1, 5):
        for o in range(OCC):
            for l in range(OCC):
                lanes = pl.ds(l * QUART, QUART)
                wbuf[4 - s, pl.ds(o, 1), lanes] = jnp.full((1, QUART), mask_ref[o, s - 1, l].astype(F32), F32)
                wsend[s - 1, pl.ds(o, 1), lanes] = jnp.full((1, QUART), mask_ref[l, s - 1, o].astype(F32), F32)
    for s in range(1, 5):
        send(("w", s), wsend.at[s - 1], wbuf.at[4 + s], at_blk(-s))
    evq = ev_ref[pl.ds(x, 1), :]
    for d in range(9):
        j = (k + nblk + d - 4) % nblk
        for o in range(OCC):
            for l in range(OCC):
                e = eo_ref[OCC * k + o] + eo_ref[OCC * j + l]
                rowb[d, pl.ds(o, 1), pl.ds(l * QUART, QUART)] = e - evq
    for h in range(2):
        row = ev_ref[pl.ds(2 * yl + h, 1), :]
        nevb[pl.ds(h * 128, 128), :] = jnp.transpose(jnp.broadcast_to(row, (128, 128)))
    acc[...] = jnp.zeros_like(acc)

    def own_ready(pr):
        local[pr].wait()
        for t in (1, 3, 2):
            arrived(("s1", pr, t), kb.at[own, pl.ds(2 * pr, 2), :, slice_of(4 - t)])
        ref = unit(own, yl, pr)
        send(("hi", pr), ref, ref, hi)
        send(("lo", pr), ref, ref, lo)
        for step in (1, -1):
            send(("z", step, pr), ref, unit(own - 4 * step, yl, pr), at_z(step))

    def to_mate(name, slot, pr):
        send((name, pr), whole(slot, pr), whole(slot, pr), mate)

    def lo_ready(pr):
        ref = unit(own, 1 - yl, pr)
        arrived(("lo", pr), ref)
        for step in (1, -1):
            send(("zz", step, pr), ref, unit(own - 4 * step, 1 - yl, pr), at_z(step))
        to_mate("mown", own, pr)

    def hi_ready(pr):
        ref = unit(cross, 1 - yl, pr)
        arrived(("hi", pr), ref)
        send(("loc", pr), ref, ref, lo)

    def z_ready(pr):
        for step in (1, -1):
            arrived(("z", step, pr), unit(own - 4 * step, yl, pr))
        ref = unit(dsend, yl, pr)
        send(("hid", pr), ref, ref, hi)

    def zz_ready(pr):
        for step in (1, -1):
            arrived(("zz", step, pr), unit(own - 4 * step, 1 - yl, pr))
        if pr == 1:
            ref = unit(dsend, 1 - yl, pr)
            send(("hie", pr), ref, ref, hi)
        to_mate("mz", zshare, pr)

    def cross_ready(pr):
        arrived(("loc", pr), unit(cross, yl, pr))
        to_mate("mcross", cross, pr)

    def hid_ready(pr):
        ref = unit(diag, 1 - yl, pr)
        arrived(("hid", pr), ref)
        if pr == 0:
            send(("lod", 0), ref, ref, lo)
        send(("md1", pr), ref, ref, mate)

    def diag_ready(pr):
        ref = unit(diag, yl, pr)
        arrived(("lod" if pr == 0 else "hie", pr), ref)
        send(("md2", pr), ref, ref, mate)

    def diag_from_mate(pr):
        arrived(("md1", pr), unit(mdiag, 1 - yl, pr))
        arrived(("md2", pr), unit(mdiag, yl, pr))

    def from_mate(name, slot, pr):
        arrived((name, pr), whole(slot, pr))

    def pick(i, values):
        value = values[-1]
        for n in range(len(values) - 2, -1, -1):
            value = jnp.where(i == n, values[n], value)
        return value

    def compute(tasks):
        def body(i, _):
            wide = len(tasks[0][0])
            rows = [slab(pick(i, [turns[n] for turns, _ in tasks])) for n in range(wide)]
            q = jnp.concatenate([qb[:, r, :].reshape(OCC * SLAB, NAUX) for r in rows], axis=0)
            nevs = [jnp.concatenate([nevb[r, :]] * 2, axis=1) for r in rows]
            total = None
            for n in range(2):
                slot = pick(i, [unit[n][0] for _, unit in tasks])
                pr = pick(i, [unit[n][1] for _, unit in tasks])
                d = slot - u
                keys = kb[slot, pl.ds(2 * pr, 2)].reshape(2 * QUART, NAUX)
                s = lax.dot_general(q, keys, (((1,), (1,)), ((), ())), preferred_element_type=F32)
                lanes = part(pr * 256, 256)
                amps = []
                for m in range(wide * OCC):
                    den = rowb[d, pl.ds(m % OCC, 1), lanes] - nevs[m // OCC]
                    w = wbuf[d, pl.ds(m % OCC, 1), lanes]
                    amps.append((s[m * SLAB : (m + 1) * SLAB] * w / den).astype(BF16))
                amp = jnp.concatenate(amps, axis=0)
                term = jnp.dot(amp, keys, preferred_element_type=F32)
                total = term if total is None else total + term
            for m in range(wide):
                acc[:, rows[m], :] += total[m * OCC * SLAB : (m + 1) * OCC * SLAB].reshape(OCC, SLAB, NAUX)
            return 0

        lax.fori_loop(0, len(tasks), body, 0)

    u0 = ((mown, 0), (mown, 1))
    u1 = ((cross, 0), (below, 0))
    u2 = ((above, 0), (mzshare, 0))
    u3 = ((mcross, 0), (cross, 1))
    u4 = ((below, 1), (above, 1))
    u5 = ((mzshare, 1), (mcross, 1))
    u6 = ((diag, 0), (diag, 1))
    u7 = ((mdiag, 0), (mdiag, 1))

    near, rest = (2, 1), (3, 0)

    own_ready(0)
    for s in range(4):
        arrived(("q1", s), qb.at[:, pl.ds(s * SLAB, SLAB), other_slice_of(0)])
    queries_other(2)
    own_ready(1)
    for turn in (1, 3, 0):
        queries(turn)
        queries_other(turn)
    lo_ready(0)
    hi_ready(0)
    z_ready(0)
    lo_ready(1)
    hi_ready(1)
    z_ready(1)
    for s in range(1, 5):
        arrived(("w", s), wbuf.at[4 + s])
    local[2].wait()
    from_mate("mown", mown, 0)
    from_mate("mown", mown, 1)
    def push(n, value, dev):
        osend[n] = value.astype(BF16)
        send(("o", n), osend.at[n], orecv.at[n], dev)

    first_two, last_two = slice(0, 2), slice(2, 4)
    queries_arrived(2)
    queries_arrived(1)
    compute([(near, u0)])
    zz_ready(0)
    cross_ready(0)
    hid_ready(0)
    compute([(near, u1)])
    from_mate("mz", mzshare, 0)
    from_mate("mcross", mcross, 0)
    compute([(near, u2)])
    zz_ready(1)
    cross_ready(1)
    hid_ready(1)
    queries_arrived(3)
    queries_arrived(0)
    compute([(rest, u0), (rest, u1)])
    from_mate("mz", mzshare, 1)
    from_mate("mcross", mcross, 1)
    compute([(near, u3), (near, u4)])
    compute([(rest, u2)])
    diag_ready(0)
    diag_ready(1)
    compute([(near, u5), (near, u6)])
    diag_from_mate(0)
    diag_from_mate(1)
    compute([(near, u7)])
    push(0, acc[first_two, slab(2), :], right)
    push(1, acc[last_two, slab(2), :], left)
    push(2, acc[last_two, slab(1), :], right)
    compute([(rest, u3), (rest, u4), (rest, u5), (rest, u6), (rest, u7)])
    push(3, acc[first_two, slab(3), :], left)
    arrived(("o", 0), orecv.at[0])
    push(4, acc[first_two, slab(1), :] + orecv[0].astype(F32), right)
    arrived(("o", 1), orecv.at[1])
    push(5, acc[last_two, slab(3), :] + orecv[1].astype(F32), left)
    for n in (2, 3):
        arrived(("o", n), orecv.at[n])
    arrived(("o", 4), orecv.at[4])
    out_ref[first_two] = acc[first_two, slab(0), :] + orecv[3].astype(F32) + orecv[4].astype(F32)
    arrived(("o", 5), orecv.at[5])
    out_ref[last_two] = acc[last_two, slab(0), :] + orecv[2].astype(F32) + orecv[5].astype(F32)
    for copy in sent:
        copy.wait_send()


def shards(integrals, eps_occ, eps_vir, pair_mask):
    vmem = pl.BlockSpec(memory_space=pltpu.VMEM)
    smem = pl.BlockSpec(memory_space=pltpu.SMEM)
    return pl.pallas_call(
        kernel,
        out_shape=pltpu.VMEM((OCC, SLAB, NAUX), F32),
        in_specs=[pl.BlockSpec(memory_space=pl.ANY), smem, vmem, smem],
        out_specs=vmem,
        scratch_shapes=[
            pltpu.VMEM((12, OCC, QUART, NAUX), BF16),
            pltpu.VMEM((OCC, HALF, NAUX), BF16),
            pltpu.VMEM((OCC, HALF, NAUX), F32),
            pltpu.VMEM((9, 8, KEYS), F32),
            pltpu.VMEM((HALF, 128), F32),
            pltpu.VMEM((9, 8, KEYS), F32),
            pltpu.VMEM((4, 8, KEYS), F32),
            pltpu.VMEM((6, 2, SLAB, NAUX), BF16),
            pltpu.VMEM((6, 2, SLAB, NAUX), BF16),
            pltpu.SemaphoreType.DMA((N_SEM,)),
            pltpu.SemaphoreType.DMA((N_SEM,)),
            pltpu.SemaphoreType.DMA((3,)),
        ],
        compiler_params=pltpu.CompilerParams(
            collective_id=0, has_side_effects=True, vmem_limit_bytes=56 * 1024 * 1024
        ),
        name="amplitudes",
    )(integrals, eps_occ, eps_vir.reshape(4, 128), pair_mask)


def solution(mesh):
    return jax.shard_map(
        shards,
        mesh=mesh,
        in_specs=(P("blk", None, "grp"), P(), P(), P("blk", None, None)),
        out_specs=P("blk", "grp", None),
        check_vma=False,
    )
```

```python
import jax
import jax.numpy as jnp
from jax import lax
from jax.experimental import pallas as pl
from jax.experimental.pallas import tpu as pltpu
from jax.sharding import PartitionSpec as P

MESH = pl.DeviceIdType.MESH
F32 = jnp.float32
BF16 = jnp.bfloat16
OCC = 4
NVIR = 512
NAUX = 1024
HALF = 256
QUART = 128
SLAB = 64
SIDE = 512
KEYS = OCC * QUART
N_SEM = 96


def kernel(
    b_ref, eo_ref, ev_ref, mask_ref, out_ref,
    kb, qb, acc, rowb, nevb, wbuf, wsend, osend, orecv, ssem, rsem, lsem,
):
    k = lax.axis_index("blk")
    g = lax.axis_index("grp")
    nblk = lax.axis_size("blk")
    u = k % 4
    z = k // 4
    nz = nblk // 4
    yh, c = u // 2, u % 2
    yl, x = g // 4, g % 4

    def at_z(step):
        return (4 * ((z + nz + step) % nz) + u, g)

    def at_x(step):
        return (k, 4 * yl + (x + step) % 4)

    def at_blk(step):
        return ((k + nblk + step) % nblk, g)

    mate = (k + 1 - 2 * c, g)
    lo = (k, 4 * (1 - yl) + x)
    hi = (4 * z + (u + 2) % 4, 4 * (1 - yl) + x)
    right, left = at_x(1), at_x(3)
    onward = (4 * ((z + nz + 1 - 2 * yh) % nz) + u, g)

    barrier = pltpu.get_barrier_semaphore()
    peers = [at_x(1), at_x(2), at_x(3), lo, hi]
    peers += [at_blk(s) for s in (1, 2, 3, 4, -1, -2, -3, -4)]
    for dev in peers:
        pl.semaphore_signal(barrier, inc=1, device_id=dev, device_id_type=MESH)
    pl.semaphore_wait(barrier, len(peers))

    sent = []
    sems = {}

    def descriptor(name, src, dst, dev):
        i = sems.setdefault(name, len(sems))
        return pltpu.make_async_remote_copy(
            src_ref=src, dst_ref=dst, send_sem=ssem.at[i], recv_sem=rsem.at[i],
            device_id=dev, device_id_type=MESH,
        )

    def send(name, src, dst, dev):
        copy = descriptor(name, src, dst, dev)
        copy.start()
        sent.append(copy)

    def arrived(name, ref):
        descriptor(name, ref, ref, mate).wait_recv()

    def part(start, size):
        return pl.ds(pl.multiple_of(start, size), size)

    own, mown = 4 + u, 5 + u - 2 * c
    mu = mown - 4
    s2, s4 = 2 - 4 * yh, 4 - 8 * yh
    below, above = u, 8 + u
    cross, mcross = own + s2, mown + s2
    diag, mdiag = own - s2, mown - s2
    dsend = own + s4
    zshare, mzshare = u + 8 * (1 - c), mu + 8 * c

    def unit(slot, half, pr):
        return kb.at[slot, pl.ds(2 * pr, 2), :, part(half * SIDE, SIDE)]

    def whole(slot, pr):
        return kb.at[slot, pl.ds(2 * pr, 2)]

    def slice_of(t):
        return part(((4 * yl) + (x + t) % 4) * 128, 128)

    def other_slice_of(t):
        return part((4 * (1 - yl) + (x + t) % 4) * 128, 128)

    cols = slice_of(0)

    local = []
    chunks = [(0, 1, 0), (1, 1, 0), (2, 2, 1)]
    for o0, n, _ in chunks:
        os = pl.ds(o0, n)
        for t in (1, 3, 2):
            rows = part((x + t) % 4 * QUART, QUART)
            send(("s1", o0, t), b_ref.at[os, rows, :], kb.at[own, os, :, cols], at_x(t))
    copy = pltpu.make_async_copy(b_ref.at[:, part(x * QUART, QUART), :], kb.at[own, :, :, cols], lsem.at[0])
    copy.start()
    local.append(copy)
    for s in range(4):
        send(("q1", s), b_ref.at[:, part((1 - yl) * HALF + s * SLAB, SLAB), :], qb.at[:, pl.ds(s * SLAB, SLAB), cols], lo)

    def slab_of(place):
        return part(place % 4 * SLAB, SLAB)

    def slab(t):
        return slab_of(x + t)

    def queries(turn):
        for t in (1, 3, 2):
            rows = part(yl * HALF + (x + t + turn) % 4 * SLAB, SLAB)
            send(("q2", turn, t), b_ref.at[:, rows, :], qb.at[:, slab_of(x + t + turn), cols], at_x(t))

    def queries_other(turn):
        for t in (1, 3, 2):
            ref = qb.at[:, slab_of(x + t + turn), other_slice_of(0)]
            send(("q3", turn, t), ref, ref, at_x(t))

    def queries_arrived(turn):
        for t in (1, 3, 2):
            arrived(("q2", turn, t), qb.at[:, slab(turn), slice_of(4 - t)])
            arrived(("q3", turn, t), qb.at[:, slab(turn), other_slice_of(4 - t)])

    queries(2)
    copy = pltpu.make_async_copy(b_ref.at[:, part(yl * HALF, HALF), :], qb.at[:, :, cols], lsem.at[1])
    copy.start()
    local.append(copy)

    for s in range(1, 5):
        for o in range(OCC):
            for l in range(OCC):
                lanes = pl.ds(l * QUART, QUART)
                wbuf[4 - s, pl.ds(o, 1), lanes] = jnp.full((1, QUART), mask_ref[o, s - 1, l].astype(F32), F32)
                wsend[s - 1, pl.ds(o, 1), lanes] = jnp.full((1, QUART), mask_ref[l, s - 1, o].astype(F32), F32)
    for s in range(1, 5):
        send(("w", s), wsend.at[s - 1], wbuf.at[4 + s], at_blk(-s))
    evq = ev_ref[pl.ds(x, 1), :]
    for d in range(9):
        j = (k + nblk + d - 4) % nblk
        for o in range(OCC):
            for l in range(OCC):
                e = eo_ref[OCC * k + o] + eo_ref[OCC * j + l]
                rowb[d, pl.ds(o, 1), pl.ds(l * QUART, QUART)] = e - evq
    for h in range(2):
        row = ev_ref[pl.ds(2 * yl + h, 1), :]
        nevb[pl.ds(h * 128, 128), :] = jnp.transpose(jnp.broadcast_to(row, (128, 128)))
    acc[...] = jnp.zeros_like(acc)

    def rows_unit(slot, half, o0, n):
        return kb.at[slot, pl.ds(o0, n), :, part(half * SIDE, SIDE)]

    def own_ready(pr):
        for o0, n, pair in chunks:
            if pair == pr:
                if o0 == 0:
                    local[0].wait()
                for t in (1, 3, 2):
                    arrived(("s1", o0, t), kb.at[own, pl.ds(o0, n), :, slice_of(4 - t)])
                ref = rows_unit(own, yl, o0, n)
                send(("hi", o0), ref, ref, hi)
                send(("lo", o0), ref, ref, lo)
                for step in (1, -1):
                    send(("z", step, o0), ref, rows_unit(own - 4 * step, yl, o0, n), at_z(step))

    def hop_arrived(name, slot, half, pr):
        for o0, n, pair in chunks:
            if pair == pr:
                arrived(name + (o0,), rows_unit(slot, half, o0, n))

    def to_mate(name, slot, pr):
        send((name, pr), whole(slot, pr), whole(slot, pr), mate)

    def lo_ready(pr):
        ref = unit(own, 1 - yl, pr)
        hop_arrived(("lo",), own, 1 - yl, pr)
        for step in (1, -1):
            send(("zz", step, pr), ref, unit(own - 4 * step, 1 - yl, pr), at_z(step))
        to_mate("mown", own, pr)

    def hi_ready(pr):
        ref = unit(cross, 1 - yl, pr)
        hop_arrived(("hi",), cross, 1 - yl, pr)
        send(("loc", pr), ref, ref, lo)

    def z_ready(pr):
        for step in (1, -1):
            hop_arrived(("z", step), own - 4 * step, yl, pr)
        ref = unit(dsend, yl, pr)
        send(("hid", pr), ref, ref, hi)

    def zz_ready(pr):
        for step in (1, -1):
            arrived(("zz", step, pr), unit(own - 4 * step, 1 - yl, pr))
        if pr == 1:
            ref = unit(dsend, 1 - yl, pr)
            send(("hie", pr), ref, ref, hi)
        to_mate("mz", zshare, pr)

    def cross_ready(pr):
        arrived(("loc", pr), unit(cross, yl, pr))
        if pr == 0:
            ref = rows_unit(cross, yl, 1, 1)
            send(("zd",), ref, rows_unit(cross - s4, yl, 1, 1), onward)
        to_mate("mcross", cross, pr)

    def hid_ready(pr):
        ref = unit(diag, 1 - yl, pr)
        arrived(("hid", pr), ref)
        if pr == 0:
            first = rows_unit(diag, 1 - yl, 0, 1)
            send(("lod", 0), first, first, lo)
        send(("md1", pr), ref, ref, mate)

    def diag_ready(pr):
        ref = unit(diag, yl, pr)
        if pr == 0:
            arrived(("lod", 0), rows_unit(diag, yl, 0, 1))
            arrived(("zd",), rows_unit(diag, yl, 1, 1))
        else:
            arrived(("hie", 1), ref)
        send(("md2", pr), ref, ref, mate)

    def diag_from_mate(pr):
        arrived(("md1", pr), unit(mdiag, 1 - yl, pr))
        arrived(("md2", pr), unit(mdiag, yl, pr))

    def from_mate(name, slot, pr):
        arrived((name, pr), whole(slot, pr))

    def pick(i, values):
        value = values[-1]
        for n in range(len(values) - 2, -1, -1):
            value = jnp.where(i == n, values[n], value)
        return value

    def compute(tasks):
        def body(i, _):
            wide = len(tasks[0][0])
            rows = [slab(pick(i, [turns[n] for turns, _ in tasks])) for n in range(wide)]
            q = jnp.concatenate([qb[:, r, :].reshape(OCC * SLAB, NAUX) for r in rows], axis=0)
            nevs = [jnp.concatenate([nevb[r, :]] * 2, axis=1) for r in rows]
            total = None
            for n in range(2):
                slot = pick(i, [unit[n][0] for _, unit in tasks])
                pr = pick(i, [unit[n][1] for _, unit in tasks])
                d = slot - u
                keys = kb[slot, pl.ds(2 * pr, 2)].reshape(2 * QUART, NAUX)
                s = lax.dot_general(q, keys, (((1,), (1,)), ((), ())), preferred_element_type=F32)
                lanes = part(pr * 256, 256)
                amps = []
                for m in range(wide * OCC):
                    den = rowb[d, pl.ds(m % OCC, 1), lanes] - nevs[m // OCC]
                    w = wbuf[d, pl.ds(m % OCC, 1), lanes]
                    amps.append((s[m * SLAB : (m + 1) * SLAB] * w / den).astype(BF16))
                amp = jnp.concatenate(amps, axis=0)
                term = jnp.dot(amp, keys, preferred_element_type=F32)
                total = term if total is None else total + term
            for m in range(wide):
                acc[:, rows[m], :] += total[m * OCC * SLAB : (m + 1) * OCC * SLAB].reshape(OCC, SLAB, NAUX)
            return 0

        lax.fori_loop(0, len(tasks), body, 0)

    u0 = ((mown, 0), (mown, 1))
    u1 = ((cross, 0), (below, 0))
    u2 = ((above, 0), (mzshare, 0))
    u3 = ((mcross, 0), (cross, 1))
    u4 = ((below, 1), (above, 1))
    u5 = ((mzshare, 1), (mcross, 1))
    u6 = ((diag, 0), (diag, 1))
    u7 = ((mdiag, 0), (mdiag, 1))

    near, rest = (2, 1), (3, 0)

    own_ready(0)
    for s in range(4):
        arrived(("q1", s), qb.at[:, pl.ds(s * SLAB, SLAB), other_slice_of(0)])
    queries_other(2)
    own_ready(1)
    for turn in (1, 3, 0):
        queries(turn)
        queries_other(turn)
    lo_ready(0)
    hi_ready(0)
    z_ready(0)
    lo_ready(1)
    hi_ready(1)
    z_ready(1)
    for s in range(1, 5):
        arrived(("w", s), wbuf.at[4 + s])
    local[1].wait()
    from_mate("mown", mown, 0)
    from_mate("mown", mown, 1)
    def push(n, value, dev):
        osend[n] = value.astype(BF16)
        send(("o", n), osend.at[n], orecv.at[n], dev)

    first_two, last_two = slice(0, 2), slice(2, 4)
    queries_arrived(2)
    queries_arrived(1)
    compute([(near, u0)])
    zz_ready(0)
    cross_ready(0)
    hid_ready(0)
    compute([(near, u1)])
    from_mate("mz", mzshare, 0)
    from_mate("mcross", mcross, 0)
    compute([(near, u2)])
    zz_ready(1)
    cross_ready(1)
    hid_ready(1)
    queries_arrived(3)
    queries_arrived(0)
    compute([(rest, u0)])
    from_mate("mz", mzshare, 1)
    from_mate("mcross", mcross, 1)
    compute([(near, u3), (near, u4)])
    diag_ready(0)
    diag_ready(1)
    compute([(near, u5), (near, u6)])
    diag_from_mate(0)
    diag_from_mate(1)
    compute([((2,), u7)])
    push(0, acc[first_two, slab(2), :], right)
    push(1, acc[last_two, slab(2), :], left)
    compute([((1,), u7)])
    push(2, acc[last_two, slab(1), :], right)
    compute([((3,), u1), ((3,), u2), ((3,), u3), ((3,), u4), ((3,), u5), ((3,), u6), ((3,), u7)])
    push(3, acc[first_two, slab(3), :], left)
    arrived(("o", 0), orecv.at[0])
    push(4, acc[first_two, slab(1), :] + orecv[0].astype(F32), right)
    arrived(("o", 1), orecv.at[1])
    push(5, acc[last_two, slab(3), :] + orecv[1].astype(F32), left)
    compute([((0,), u1), ((0,), u2), ((0,), u3), ((0,), u4), ((0,), u5), ((0,), u6), ((0,), u7)])
    for n in (2, 3):
        arrived(("o", n), orecv.at[n])
    arrived(("o", 4), orecv.at[4])
    out_ref[first_two] = acc[first_two, slab(0), :] + orecv[3].astype(F32) + orecv[4].astype(F32)
    arrived(("o", 5), orecv.at[5])
    out_ref[last_two] = acc[last_two, slab(0), :] + orecv[2].astype(F32) + orecv[5].astype(F32)
    for copy in sent:
        copy.wait_send()


def shards(integrals, eps_occ, eps_vir, pair_mask):
    vmem = pl.BlockSpec(memory_space=pltpu.VMEM)
    smem = pl.BlockSpec(memory_space=pltpu.SMEM)
    return pl.pallas_call(
        kernel,
        out_shape=pltpu.VMEM((OCC, SLAB, NAUX), F32),
        in_specs=[pl.BlockSpec(memory_space=pl.ANY), smem, vmem, smem],
        out_specs=vmem,
        scratch_shapes=[
            pltpu.VMEM((12, OCC, QUART, NAUX), BF16),
            pltpu.VMEM((OCC, HALF, NAUX), BF16),
            pltpu.VMEM((OCC, HALF, NAUX), F32),
            pltpu.VMEM((9, 8, KEYS), F32),
            pltpu.VMEM((HALF, 128), F32),
            pltpu.VMEM((9, 8, KEYS), F32),
            pltpu.VMEM((4, 8, KEYS), F32),
            pltpu.VMEM((6, 2, SLAB, NAUX), BF16),
            pltpu.VMEM((6, 2, SLAB, NAUX), BF16),
            pltpu.SemaphoreType.DMA((N_SEM,)),
            pltpu.SemaphoreType.DMA((N_SEM,)),
            pltpu.SemaphoreType.DMA((2,)),
        ],
        compiler_params=pltpu.CompilerParams(
            collective_id=0, has_side_effects=True, vmem_limit_bytes=56 * 1024 * 1024
        ),
        name="amplitudes",
    )(integrals, eps_occ, eps_vir.reshape(4, 128), pair_mask)


def solution(mesh):
    return jax.shard_map(
        shards,
        mesh=mesh,
        in_specs=(P("blk", None, "grp"), P(), P(), P("blk", None, None)),
        out_specs=P("blk", "grp", None),
        check_vma=False,
    )
```

```python
import jax
import jax.numpy as jnp
from jax import lax
from jax.experimental import pallas as pl
from jax.experimental.pallas import tpu as pltpu
from jax.sharding import PartitionSpec as P

MESH = pl.DeviceIdType.MESH
F32 = jnp.float32
BF16 = jnp.bfloat16
OCC = 4
NVIR = 512
NAUX = 1024
HALF = 256
QUART = 128
SLAB = 64
SIDE = 512
KEYS = OCC * QUART
N_SEM = 96


def kernel(
    b_ref, eo_ref, ev_ref, mask_ref, out_ref,
    kb, qb, acc, rowb, nevb, wbuf, wsend, osend, orecv, ssem, rsem, lsem,
):
    k = lax.axis_index("blk")
    g = lax.axis_index("grp")
    nblk = lax.axis_size("blk")
    u = k % 4
    z = k // 4
    nz = nblk // 4
    yh, c = u // 2, u % 2
    yl, x = g // 4, g % 4

    def at_z(step):
        return (4 * ((z + nz + step) % nz) + u, g)

    def at_x(step):
        return (k, 4 * yl + (x + step) % 4)

    def at_blk(step):
        return ((k + nblk + step) % nblk, g)

    mate = (k + 1 - 2 * c, g)
    lo = (k, 4 * (1 - yl) + x)
    hi = (4 * z + (u + 2) % 4, 4 * (1 - yl) + x)
    right, left = at_x(1), at_x(3)
    onward = (4 * ((z + nz + 1 - 2 * yh) % nz) + u, g)

    barrier = pltpu.get_barrier_semaphore()
    peers = [at_x(1), at_x(2), at_x(3), lo, hi]
    peers += [at_blk(s) for s in (1, 2, 3, 4, -1, -2, -3, -4)]
    for dev in peers:
        pl.semaphore_signal(barrier, inc=1, device_id=dev, device_id_type=MESH)
    pl.semaphore_wait(barrier, len(peers))

    sent = []
    sems = {}

    def descriptor(name, src, dst, dev):
        i = sems.setdefault(name, len(sems))
        return pltpu.make_async_remote_copy(
            src_ref=src, dst_ref=dst, send_sem=ssem.at[i], recv_sem=rsem.at[i],
            device_id=dev, device_id_type=MESH,
        )

    def send(name, src, dst, dev):
        copy = descriptor(name, src, dst, dev)
        copy.start()
        sent.append(copy)

    def arrived(name, ref):
        descriptor(name, ref, ref, mate).wait_recv()

    def part(start, size):
        return pl.ds(pl.multiple_of(start, size), size)

    own, mown = 4 + u, 5 + u - 2 * c
    mu = mown - 4
    s2, s4 = 2 - 4 * yh, 4 - 8 * yh
    below, above = u, 8 + u
    cross, mcross = own + s2, mown + s2
    diag, mdiag = own - s2, mown - s2
    dsend = own + s4
    zshare, mzshare = u + 8 * (1 - c), mu + 8 * c

    def unit(slot, half, pr):
        return kb.at[slot, pl.ds(2 * pr, 2), :, part(half * SIDE, SIDE)]

    def whole(slot, pr):
        return kb.at[slot, pl.ds(2 * pr, 2)]

    def slice_of(t):
        return part(((4 * yl) + (x + t) % 4) * 128, 128)

    def other_slice_of(t):
        return part((4 * (1 - yl) + (x + t) % 4) * 128, 128)

    cols = slice_of(0)

    local = []
    chunks = [(0, 1, 0), (1, 1, 0), (2, 2, 1)]
    for o0, n, _ in chunks:
        os = pl.ds(o0, n)
        for t in (1, 3, 2):
            rows = part((x + t) % 4 * QUART, QUART)
            send(("s1", o0, t), b_ref.at[os, rows, :], kb.at[own, os, :, cols], at_x(t))
    copy = pltpu.make_async_copy(b_ref.at[:, part(x * QUART, QUART), :], kb.at[own, :, :, cols], lsem.at[0])
    copy.start()
    local.append(copy)
    for s in range(4):
        send(("q1", s), b_ref.at[:, part((1 - yl) * HALF + s * SLAB, SLAB), :], qb.at[:, pl.ds(s * SLAB, SLAB), cols], lo)

    def slab_of(place):
        return part(place % 4 * SLAB, SLAB)

    def slab(t):
        return slab_of(x + t)

    def queries(turn):
        for t in (1, 3, 2):
            rows = part(yl * HALF + (x + t + turn) % 4 * SLAB, SLAB)
            send(("q2", turn, t), b_ref.at[:, rows, :], qb.at[:, slab_of(x + t + turn), cols], at_x(t))

    def queries_other(turn):
        for t in (1, 3, 2):
            ref = qb.at[:, slab_of(x + t + turn), other_slice_of(0)]
            send(("q3", turn, t), ref, ref, at_x(t))

    def queries_arrived(turn):
        for t in (1, 3, 2):
            arrived(("q2", turn, t), qb.at[:, slab(turn), slice_of(4 - t)])
            arrived(("q3", turn, t), qb.at[:, slab(turn), other_slice_of(4 - t)])

    queries(2)
    copy = pltpu.make_async_copy(b_ref.at[:, part(yl * HALF, HALF), :], qb.at[:, :, cols], lsem.at[1])
    copy.start()
    local.append(copy)

    for s in range(1, 5):
        for o in range(OCC):
            for l in range(OCC):
                lanes = pl.ds(l * QUART, QUART)
                wbuf[4 - s, pl.ds(o, 1), lanes] = jnp.full((1, QUART), mask_ref[o, s - 1, l].astype(F32), F32)
                wsend[s - 1, pl.ds(o, 1), lanes] = jnp.full((1, QUART), mask_ref[l, s - 1, o].astype(F32), F32)
    for s in range(1, 5):
        send(("w", s), wsend.at[s - 1], wbuf.at[4 + s], at_blk(-s))
    evq = ev_ref[pl.ds(x, 1), :]
    for d in range(9):
        j = (k + nblk + d - 4) % nblk
        for o in range(OCC):
            for l in range(OCC):
                e = eo_ref[OCC * k + o] + eo_ref[OCC * j + l]
                rowb[d, pl.ds(o, 1), pl.ds(l * QUART, QUART)] = e - evq
    for h in range(2):
        row = ev_ref[pl.ds(2 * yl + h, 1), :]
        nevb[pl.ds(h * 128, 128), :] = jnp.transpose(jnp.broadcast_to(row, (128, 128)))
    acc[...] = jnp.zeros_like(acc)

    def rows_unit(slot, half, o0, n):
        return kb.at[slot, pl.ds(o0, n), :, part(half * SIDE, SIDE)]

    def own_ready(pr):
        for o0, n, pair in chunks:
            if pair == pr:
                if o0 == 0:
                    local[0].wait()
                for t in (1, 3, 2):
                    arrived(("s1", o0, t), kb.at[own, pl.ds(o0, n), :, slice_of(4 - t)])
                ref = rows_unit(own, yl, o0, n)
                send(("hi", o0), ref, ref, hi)
                send(("lo", o0), ref, ref, lo)
                for step in (1, -1):
                    send(("z", step, o0), ref, rows_unit(own - 4 * step, yl, o0, n), at_z(step))

    def hop_arrived(name, slot, half, pr):
        for o0, n, pair in chunks:
            if pair == pr:
                arrived(name + (o0,), rows_unit(slot, half, o0, n))

    def to_mate(name, slot, pr):
        send((name, pr), whole(slot, pr), whole(slot, pr), mate)

    def lo_ready(pr):
        ref = unit(own, 1 - yl, pr)
        hop_arrived(("lo",), own, 1 - yl, pr)
        for step in (1, -1):
            send(("zz", step, pr), ref, unit(own - 4 * step, 1 - yl, pr), at_z(step))
        to_mate("mown", own, pr)

    def hi_ready(pr):
        ref = unit(cross, 1 - yl, pr)
        hop_arrived(("hi",), cross, 1 - yl, pr)
        send(("loc", pr), ref, ref, lo)

    def z_ready(pr):
        for step in (1, -1):
            hop_arrived(("z", step), own - 4 * step, yl, pr)
        ref = unit(dsend, yl, pr)
        send(("hid", pr), ref, ref, hi)

    def zz_ready(pr):
        for step in (1, -1):
            arrived(("zz", step, pr), unit(own - 4 * step, 1 - yl, pr))
        if pr == 1:
            ref = unit(dsend, 1 - yl, pr)
            send(("hie", pr), ref, ref, hi)
        to_mate("mz", zshare, pr)

    def cross_ready(pr):
        arrived(("loc", pr), unit(cross, yl, pr))
        if pr == 0:
            ref = rows_unit(cross, yl, 1, 1)
            send(("zd",), ref, rows_unit(cross - s4, yl, 1, 1), onward)
        to_mate("mcross", cross, pr)

    def hid_ready(pr):
        ref = unit(diag, 1 - yl, pr)
        arrived(("hid", pr), ref)
        if pr == 0:
            first = rows_unit(diag, 1 - yl, 0, 1)
            send(("lod", 0), first, first, lo)
        send(("md1", pr), ref, ref, mate)

    def diag_ready(pr):
        ref = unit(diag, yl, pr)
        if pr == 0:
            arrived(("lod", 0), rows_unit(diag, yl, 0, 1))
            arrived(("zd",), rows_unit(diag, yl, 1, 1))
        else:
            arrived(("hie", 1), ref)
        send(("md2", pr), ref, ref, mate)

    def diag_from_mate(pr):
        arrived(("md1", pr), unit(mdiag, 1 - yl, pr))
        arrived(("md2", pr), unit(mdiag, yl, pr))

    def from_mate(name, slot, pr):
        arrived((name, pr), whole(slot, pr))

    def pick(i, values):
        value = values[-1]
        for n in range(len(values) - 2, -1, -1):
            value = jnp.where(i == n, values[n], value)
        return value

    def compute(tasks):
        def body(i, _):
            wide = len(tasks[0][0])
            rows = [slab(pick(i, [turns[n] for turns, _ in tasks])) for n in range(wide)]
            q = jnp.concatenate([qb[:, r, :].reshape(OCC * SLAB, NAUX) for r in rows], axis=0)
            nevs = [jnp.concatenate([nevb[r, :]] * 2, axis=1) for r in rows]
            total = None
            for n in range(2):
                slot = pick(i, [unit[n][0] for _, unit in tasks])
                pr = pick(i, [unit[n][1] for _, unit in tasks])
                d = slot - u
                keys = kb[slot, pl.ds(2 * pr, 2)].reshape(2 * QUART, NAUX)
                s = lax.dot_general(q, keys, (((1,), (1,)), ((), ())), preferred_element_type=F32)
                lanes = part(pr * 256, 256)
                amps = []
                for m in range(wide * OCC):
                    den = rowb[d, pl.ds(m % OCC, 1), lanes] - nevs[m // OCC]
                    w = wbuf[d, pl.ds(m % OCC, 1), lanes]
                    amps.append((s[m * SLAB : (m + 1) * SLAB] * w / den).astype(BF16))
                amp = jnp.concatenate(amps, axis=0)
                term = jnp.dot(amp, keys, preferred_element_type=F32)
                total = term if total is None else total + term
            for m in range(wide):
                acc[:, rows[m], :] += total[m * OCC * SLAB : (m + 1) * OCC * SLAB].reshape(OCC, SLAB, NAUX)
            return 0

        lax.fori_loop(0, len(tasks), body, 0)

    u0 = ((mown, 0), (mown, 1))
    u1 = ((cross, 0), (below, 0))
    u2 = ((above, 0), (mzshare, 0))
    u3 = ((mcross, 0), (cross, 1))
    u4 = ((below, 1), (above, 1))
    u5 = ((mzshare, 1), (mcross, 1))
    u6 = ((diag, 0), (diag, 1))
    u7 = ((mdiag, 0), (mdiag, 1))

    own_ready(0)
    for s in range(4):
        arrived(("q1", s), qb.at[:, pl.ds(s * SLAB, SLAB), other_slice_of(0)])
    queries_other(2)
    own_ready(1)
    for turn in (1, 3, 0):
        queries(turn)
        queries_other(turn)
    lo_ready(0)
    hi_ready(0)
    z_ready(0)
    lo_ready(1)
    hi_ready(1)
    z_ready(1)
    for s in range(1, 5):
        arrived(("w", s), wbuf.at[4 + s])
    local[1].wait()
    from_mate("mown", mown, 0)
    from_mate("mown", mown, 1)
    def push(n, value, dev):
        osend[n] = value.astype(BF16)
        send(("o", n), osend.at[n], orecv.at[n], dev)

    first_two, last_two = slice(0, 2), slice(2, 4)
    queries_arrived(2)
    queries_arrived(1)
    compute([((2, 1), u0)])
    zz_ready(0)
    cross_ready(0)
    hid_ready(0)
    compute([((2, 1), u1)])
    from_mate("mz", mzshare, 0)
    from_mate("mcross", mcross, 0)
    compute([((2, 1), u2)])
    zz_ready(1)
    cross_ready(1)
    hid_ready(1)
    queries_arrived(3)
    compute([((3,), u0), ((3,), u1)])
    from_mate("mz", mzshare, 1)
    from_mate("mcross", mcross, 1)
    compute([((2, 1), u3)])
    compute([((2,), u4)])
    compute([((3,), u2)])
    diag_ready(0)
    diag_ready(1)
    compute([((2,), u5), ((2,), u6)])
    diag_from_mate(0)
    diag_from_mate(1)
    compute([((2,), u7)])
    push(0, acc[first_two, slab(2), :], right)
    push(1, acc[last_two, slab(2), :], left)
    compute([((1, 3), u5), ((1, 3), u6), ((1, 3), u7)])
    compute([((1,), u4)])
    push(2, acc[last_two, slab(1), :], right)
    compute([((3,), u3), ((3,), u4)])
    push(3, acc[first_two, slab(3), :], left)
    arrived(("o", 0), orecv.at[0])
    push(4, acc[first_two, slab(1), :] + orecv[0].astype(F32), right)
    arrived(("o", 1), orecv.at[1])
    push(5, acc[last_two, slab(3), :] + orecv[1].astype(F32), left)
    queries_arrived(0)
    compute([((0,), u0), ((0,), u1), ((0,), u2), ((0,), u3), ((0,), u4), ((0,), u5), ((0,), u6), ((0,), u7)])
    for n in (2, 3):
        arrived(("o", n), orecv.at[n])
    arrived(("o", 4), orecv.at[4])
    out_ref[first_two] = acc[first_two, slab(0), :] + orecv[3].astype(F32) + orecv[4].astype(F32)
    arrived(("o", 5), orecv.at[5])
    out_ref[last_two] = acc[last_two, slab(0), :] + orecv[2].astype(F32) + orecv[5].astype(F32)
    for copy in sent:
        copy.wait_send()


def shards(integrals, eps_occ, eps_vir, pair_mask):
    vmem = pl.BlockSpec(memory_space=pltpu.VMEM)
    smem = pl.BlockSpec(memory_space=pltpu.SMEM)
    return pl.pallas_call(
        kernel,
        out_shape=pltpu.VMEM((OCC, SLAB, NAUX), F32),
        in_specs=[pl.BlockSpec(memory_space=pl.ANY), smem, vmem, smem],
        out_specs=vmem,
        scratch_shapes=[
            pltpu.VMEM((12, OCC, QUART, NAUX), BF16),
            pltpu.VMEM((OCC, HALF, NAUX), BF16),
            pltpu.VMEM((OCC, HALF, NAUX), F32),
            pltpu.VMEM((9, 8, KEYS), F32),
            pltpu.VMEM((HALF, 128), F32),
            pltpu.VMEM((9, 8, KEYS), F32),
            pltpu.VMEM((4, 8, KEYS), F32),
            pltpu.VMEM((6, 2, SLAB, NAUX), BF16),
            pltpu.VMEM((6, 2, SLAB, NAUX), BF16),
            pltpu.SemaphoreType.DMA((N_SEM,)),
            pltpu.SemaphoreType.DMA((N_SEM,)),
            pltpu.SemaphoreType.DMA((2,)),
        ],
        compiler_params=pltpu.CompilerParams(
            collective_id=0, has_side_effects=True, vmem_limit_bytes=56 * 1024 * 1024
        ),
        name="amplitudes",
    )(integrals, eps_occ, eps_vir.reshape(4, 128), pair_mask)


def solution(mesh):
    return jax.shard_map(
        shards,
        mesh=mesh,
        in_specs=(P("blk", None, "grp"), P(), P(), P("blk", None, None)),
        out_specs=P("blk", "grp", None),
        check_vma=False,
    )
```

```python
import jax
import jax.numpy as jnp
from jax import lax
from jax.experimental import pallas as pl
from jax.experimental.pallas import tpu as pltpu
from jax.sharding import PartitionSpec as P

MESH = pl.DeviceIdType.MESH
F32 = jnp.float32
BF16 = jnp.bfloat16
OCC = 4
NVIR = 512
NAUX = 1024
HALF = 256
QUART = 128
SLAB = 64
SIDE = 512
KEYS = OCC * QUART
N_SEM = 96


def kernel(
    b_ref, eo_ref, ev_ref, mask_ref, out_ref,
    kb, qb, acc, rowb, nevb, wbuf, wsend, osend, orecv, ssem, rsem, lsem,
):
    k = lax.axis_index("blk")
    g = lax.axis_index("grp")
    nblk = lax.axis_size("blk")
    u = k % 4
    z = k // 4
    nz = nblk // 4
    yh, c = u // 2, u % 2
    yl, x = g // 4, g % 4

    def at_z(step):
        return (4 * ((z + nz + step) % nz) + u, g)

    def at_x(step):
        return (k, 4 * yl + (x + step) % 4)

    def at_blk(step):
        return ((k + nblk + step) % nblk, g)

    mate = (k + 1 - 2 * c, g)
    lo = (k, 4 * (1 - yl) + x)
    hi = (4 * z + (u + 2) % 4, 4 * (1 - yl) + x)
    right, left = at_x(1), at_x(3)
    onward = (4 * ((z + nz + 1 - 2 * yh) % nz) + u, g)

    barrier = pltpu.get_barrier_semaphore()
    peers = [at_x(1), at_x(2), at_x(3), lo, hi]
    peers += [at_blk(s) for s in (1, 2, 3, 4, -1, -2, -3, -4)]
    for dev in peers:
        pl.semaphore_signal(barrier, inc=1, device_id=dev, device_id_type=MESH)
    pl.semaphore_wait(barrier, len(peers))

    sent = []
    sems = {}

    def descriptor(name, src, dst, dev):
        i = sems.setdefault(name, len(sems))
        return pltpu.make_async_remote_copy(
            src_ref=src, dst_ref=dst, send_sem=ssem.at[i], recv_sem=rsem.at[i],
            device_id=dev, device_id_type=MESH,
        )

    def send(name, src, dst, dev):
        copy = descriptor(name, src, dst, dev)
        copy.start()
        sent.append(copy)

    def arrived(name, ref):
        descriptor(name, ref, ref, mate).wait_recv()

    def part(start, size):
        return pl.ds(pl.multiple_of(start, size), size)

    own, mown = 4 + u, 5 + u - 2 * c
    mu = mown - 4
    s2, s4 = 2 - 4 * yh, 4 - 8 * yh
    below, above = u, 8 + u
    cross, mcross = own + s2, mown + s2
    diag, mdiag = own - s2, mown - s2
    dsend = own + s4
    zshare, mzshare = u + 8 * (1 - c), mu + 8 * c

    def unit(slot, half, pr):
        return kb.at[slot, pl.ds(2 * pr, 2), :, part(half * SIDE, SIDE)]

    def whole(slot, pr):
        return kb.at[slot, pl.ds(2 * pr, 2)]

    def slice_of(t):
        return part(((4 * yl) + (x + t) % 4) * 128, 128)

    def other_slice_of(t):
        return part((4 * (1 - yl) + (x + t) % 4) * 128, 128)

    cols = slice_of(0)

    local = []
    chunks = [(0, 1, 0), (1, 1, 0), (2, 2, 1)]
    for o0, n, _ in chunks:
        os = pl.ds(o0, n)
        for t in (1, 3, 2):
            rows = part((x + t) % 4 * QUART, QUART)
            send(("s1", o0, t), b_ref.at[os, rows, :], kb.at[own, os, :, cols], at_x(t))
    copy = pltpu.make_async_copy(b_ref.at[:, part(x * QUART, QUART), :], kb.at[own, :, :, cols], lsem.at[0])
    copy.start()
    local.append(copy)
    for s in range(4):
        send(("q1", s), b_ref.at[:, part((1 - yl) * HALF + s * SLAB, SLAB), :], qb.at[:, pl.ds(s * SLAB, SLAB), cols], lo)

    def slab_of(place):
        return part(place % 4 * SLAB, SLAB)

    def slab(t):
        return slab_of(x + t)

    def queries(turn):
        for t in (1, 3, 2):
            rows = part(yl * HALF + (x + t + turn) % 4 * SLAB, SLAB)
            send(("q2", turn, t), b_ref.at[:, rows, :], qb.at[:, slab_of(x + t + turn), cols], at_x(t))

    def queries_other(turn):
        for t in (1, 3, 2):
            ref = qb.at[:, slab_of(x + t + turn), other_slice_of(0)]
            send(("q3", turn, t), ref, ref, at_x(t))

    def queries_arrived(turn):
        for t in (1, 3, 2):
            arrived(("q2", turn, t), qb.at[:, slab(turn), slice_of(4 - t)])
            arrived(("q3", turn, t), qb.at[:, slab(turn), other_slice_of(4 - t)])

    queries(2)
    copy = pltpu.make_async_copy(b_ref.at[:, part(yl * HALF, HALF), :], qb.at[:, :, cols], lsem.at[1])
    copy.start()
    local.append(copy)

    for s in range(1, 5):
        for o in range(OCC):
            for l in range(OCC):
                lanes = pl.ds(l * QUART, QUART)
                wbuf[4 - s, pl.ds(o, 1), lanes] = jnp.full((1, QUART), mask_ref[o, s - 1, l].astype(F32), F32)
                wsend[s - 1, pl.ds(o, 1), lanes] = jnp.full((1, QUART), mask_ref[l, s - 1, o].astype(F32), F32)
    for s in range(1, 5):
        send(("w", s), wsend.at[s - 1], wbuf.at[4 + s], at_blk(-s))
    evq = ev_ref[pl.ds(x, 1), :]
    for d in range(9):
        j = (k + nblk + d - 4) % nblk
        for o in range(OCC):
            for l in range(OCC):
                e = eo_ref[OCC * k + o] + eo_ref[OCC * j + l]
                rowb[d, pl.ds(o, 1), pl.ds(l * QUART, QUART)] = e - evq
    for h in range(2):
        row = ev_ref[pl.ds(2 * yl + h, 1), :]
        nevb[pl.ds(h * 128, 128), :] = jnp.transpose(jnp.broadcast_to(row, (128, 128)))
    acc[...] = jnp.zeros_like(acc)

    def rows_unit(slot, half, o0, n):
        return kb.at[slot, pl.ds(o0, n), :, part(half * SIDE, SIDE)]

    def own_ready(pr):
        for o0, n, pair in chunks:
            if pair == pr:
                if o0 == 0:
                    local[0].wait()
                for t in (1, 3, 2):
                    arrived(("s1", o0, t), kb.at[own, pl.ds(o0, n), :, slice_of(4 - t)])
                ref = rows_unit(own, yl, o0, n)
                send(("hi", o0), ref, ref, hi)
                send(("lo", o0), ref, ref, lo)
                for step in (1, -1):
                    send(("z", step, o0), ref, rows_unit(own - 4 * step, yl, o0, n), at_z(step))

    def hop_arrived(name, slot, half, pr):
        for o0, n, pair in chunks:
            if pair == pr:
                arrived(name + (o0,), rows_unit(slot, half, o0, n))

    def to_mate(name, slot, pr):
        send((name, pr), whole(slot, pr), whole(slot, pr), mate)

    def lo_ready(pr):
        ref = unit(own, 1 - yl, pr)
        hop_arrived(("lo",), own, 1 - yl, pr)
        for step in (1, -1):
            send(("zz", step, pr), ref, unit(own - 4 * step, 1 - yl, pr), at_z(step))
        to_mate("mown", own, pr)

    def hi_ready(pr):
        ref = unit(cross, 1 - yl, pr)
        hop_arrived(("hi",), cross, 1 - yl, pr)
        send(("loc", pr), ref, ref, lo)

    def z_ready(pr):
        for step in (1, -1):
            hop_arrived(("z", step), own - 4 * step, yl, pr)
        ref = unit(dsend, yl, pr)
        send(("hid", pr), ref, ref, hi)

    def zz_ready(pr):
        for step in (1, -1):
            arrived(("zz", step, pr), unit(own - 4 * step, 1 - yl, pr))
        if pr == 1:
            ref = unit(dsend, 1 - yl, pr)
            send(("hie", pr), ref, ref, hi)
        to_mate("mz", zshare, pr)

    def cross_ready(pr):
        arrived(("loc", pr), unit(cross, yl, pr))
        if pr == 0:
            ref = rows_unit(cross, yl, 1, 1)
            send(("zd",), ref, rows_unit(cross - s4, yl, 1, 1), onward)
        to_mate("mcross", cross, pr)

    def hid_ready(pr):
        ref = unit(diag, 1 - yl, pr)
        arrived(("hid", pr), ref)
        if pr == 0:
            first = rows_unit(diag, 1 - yl, 0, 1)
            send(("lod", 0), first, first, lo)
        send(("md1", pr), ref, ref, mate)

    def diag_ready(pr):
        ref = unit(diag, yl, pr)
        if pr == 0:
            arrived(("lod", 0), rows_unit(diag, yl, 0, 1))
            arrived(("zd",), rows_unit(diag, yl, 1, 1))
        else:
            arrived(("hie", 1), ref)
        send(("md2", pr), ref, ref, mate)

    def diag_from_mate(pr):
        arrived(("md1", pr), unit(mdiag, 1 - yl, pr))
        arrived(("md2", pr), unit(mdiag, yl, pr))

    def from_mate(name, slot, pr):
        arrived((name, pr), whole(slot, pr))

    def pick(i, values):
        value = values[-1]
        for n in range(len(values) - 2, -1, -1):
            value = jnp.where(i == n, values[n], value)
        return value

    def compute(tasks):
        def body(i, _):
            wide = len(tasks[0][0])
            rows = [slab(pick(i, [turns[n] for turns, _ in tasks])) for n in range(wide)]
            q = jnp.concatenate([qb[:, r, :].reshape(OCC * SLAB, NAUX) for r in rows], axis=0)
            nevs = [jnp.concatenate([nevb[r, :]] * 2, axis=1) for r in rows]
            total = None
            for n in range(2):
                slot = pick(i, [unit[n][0] for _, unit in tasks])
                pr = pick(i, [unit[n][1] for _, unit in tasks])
                d = slot - u
                keys = kb[slot, pl.ds(2 * pr, 2)].reshape(2 * QUART, NAUX)
                s = lax.dot_general(q, keys, (((1,), (1,)), ((), ())), preferred_element_type=F32)
                lanes = part(pr * 256, 256)
                amps = []
                for m in range(wide * OCC):
                    den = rowb[d, pl.ds(m % OCC, 1), lanes] - nevs[m // OCC]
                    w = wbuf[d, pl.ds(m % OCC, 1), lanes]
                    amps.append((s[m * SLAB : (m + 1) * SLAB] * w / den).astype(BF16))
                amp = jnp.concatenate(amps, axis=0)
                term = jnp.dot(amp, keys, preferred_element_type=F32)
                total = term if total is None else total + term
            for m in range(wide):
                acc[:, rows[m], :] += total[m * OCC * SLAB : (m + 1) * OCC * SLAB].reshape(OCC, SLAB, NAUX)
            return 0

        lax.fori_loop(0, len(tasks), body, 0)

    u0 = ((mown, 0), (mown, 1))
    u1 = ((cross, 0), (below, 0))
    u2 = ((above, 0), (mzshare, 0))
    u3 = ((mcross, 0), (cross, 1))
    u4 = ((below, 1), (above, 1))
    u5 = ((mzshare, 1), (mcross, 1))
    u6 = ((diag, 0), (diag, 1))
    u7 = ((mdiag, 0), (mdiag, 1))

    own_ready(0)
    for s in range(4):
        arrived(("q1", s), qb.at[:, pl.ds(s * SLAB, SLAB), other_slice_of(0)])
    queries_other(2)
    own_ready(1)
    for turn in (1, 3, 0):
        queries(turn)
        queries_other(turn)
    lo_ready(0)
    hi_ready(0)
    z_ready(0)
    lo_ready(1)
    hi_ready(1)
    z_ready(1)
    for s in range(1, 5):
        arrived(("w", s), wbuf.at[4 + s])
    local[1].wait()
    from_mate("mown", mown, 0)
    from_mate("mown", mown, 1)
    def push(n, value, dev):
        osend[n] = value.astype(BF16)
        send(("o", n), osend.at[n], orecv.at[n], dev)

    first_two, last_two = slice(0, 2), slice(2, 4)
    queries_arrived(2)
    queries_arrived(1)
    compute([((2, 1), u0)])
    zz_ready(0)
    cross_ready(0)
    hid_ready(0)
    compute([((2, 1), u1)])
    from_mate("mz", mzshare, 0)
    from_mate("mcross", mcross, 0)
    compute([((2, 1), u2)])
    zz_ready(1)
    cross_ready(1)
    hid_ready(1)
    queries_arrived(3)
    compute([((3,), u0), ((3,), u1)])
    from_mate("mz", mzshare, 1)
    from_mate("mcross", mcross, 1)
    compute([((2, 1), u3)])
    compute([((2,), u4)])
    compute([((3,), u2)])
    diag_ready(0)
    diag_ready(1)
    compute([((2,), u5), ((2,), u6)])
    diag_from_mate(0)
    diag_from_mate(1)
    compute([((2,), u7)])
    push(0, acc[first_two, slab(2), :], right)
    push(1, acc[last_two, slab(2), :], left)
    compute([((1, 3), u5), ((1, 3), u6), ((1, 3), u7)])
    compute([((1,), u4)])
    push(2, acc[last_two, slab(1), :], right)
    compute([((3,), u3), ((3,), u4)])
    push(3, acc[first_two, slab(3), :], left)
    arrived(("o", 0), orecv.at[0])
    for r in range(2):
        osend[4, r] = (acc[r, slab(1), :] + orecv[0, r].astype(F32)).astype(BF16)
        send(("b", 4, r), osend.at[4, r], orecv.at[4, r], right)
    arrived(("o", 1), orecv.at[1])
    for r in range(2):
        osend[5, r] = (acc[2 + r, slab(3), :] + orecv[1, r].astype(F32)).astype(BF16)
        send(("b", 5, r), osend.at[5, r], orecv.at[5, r], left)
    queries_arrived(0)
    compute([((0,), u0), ((0,), u1), ((0,), u2), ((0,), u3), ((0,), u4), ((0,), u5), ((0,), u6), ((0,), u7)])
    for n in (2, 3):
        arrived(("o", n), orecv.at[n])
    out_ref[first_two] = acc[first_two, slab(0), :] + orecv[3].astype(F32)
    out_ref[last_two] = acc[last_two, slab(0), :] + orecv[2].astype(F32)
    for r in range(2):
        for n, o in ((4, r), (5, 2 + r)):
            arrived(("b", n, r), orecv.at[n, r])
            out_ref[o] = out_ref[o] + orecv[n, r].astype(F32)
    for copy in sent:
        copy.wait_send()


def shards(integrals, eps_occ, eps_vir, pair_mask):
    vmem = pl.BlockSpec(memory_space=pltpu.VMEM)
    smem = pl.BlockSpec(memory_space=pltpu.SMEM)
    return pl.pallas_call(
        kernel,
        out_shape=pltpu.VMEM((OCC, SLAB, NAUX), F32),
        in_specs=[pl.BlockSpec(memory_space=pl.ANY), smem, vmem, smem],
        out_specs=vmem,
        scratch_shapes=[
            pltpu.VMEM((12, OCC, QUART, NAUX), BF16),
            pltpu.VMEM((OCC, HALF, NAUX), BF16),
            pltpu.VMEM((OCC, HALF, NAUX), F32),
            pltpu.VMEM((9, 8, KEYS), F32),
            pltpu.VMEM((HALF, 128), F32),
            pltpu.VMEM((9, 8, KEYS), F32),
            pltpu.VMEM((4, 8, KEYS), F32),
            pltpu.VMEM((6, 2, SLAB, NAUX), BF16),
            pltpu.VMEM((6, 2, SLAB, NAUX), BF16),
            pltpu.SemaphoreType.DMA((N_SEM,)),
            pltpu.SemaphoreType.DMA((N_SEM,)),
            pltpu.SemaphoreType.DMA((2,)),
        ],
        compiler_params=pltpu.CompilerParams(
            collective_id=0, has_side_effects=True, vmem_limit_bytes=56 * 1024 * 1024
        ),
        name="amplitudes",
    )(integrals, eps_occ, eps_vir.reshape(4, 128), pair_mask)


def solution(mesh):
    return jax.shard_map(
        shards,
        mesh=mesh,
        in_specs=(P("blk", None, "grp"), P(), P(), P("blk", None, None)),
        out_specs=P("blk", "grp", None),
        check_vma=False,
    )
```
